256 devices in a mesh: area: 16 (over x, y), sec: 16 (over z, core).
Axes of the slice: x: 4, y: 4, z: 8, core: 2. Of those that a mesh axis runs over, the one named last changes fastest.
Arguments:
- spikes: int32 [16, 3, 16384], P('area', None, 'sec'), may hold values 0 or 1
- intra_weight: float32 [16, 128, 8, 128, 128], P('area', 'sec'), may hold values from -0.5 to 0.5
- intra_dest: int32 [16, 128, 8], P('area'), may hold values from 0 to 127, all different within a row
- inter_weight: float32 [16, 128, 2, 128, 128], P('area', 'sec'), may hold values from -0.5 to 0.5
- inter_target: int32 [16, 16, 2], P(None, 'sec'), may hold values from 0 to 15, all different within a row
- v_init: float32 [16, 16384], P('area', 'sec'), may hold values from 0 to 1
- leak: float32 [16, 16384], P('area', 'sec'), may hold values from 0.3 to 0.95
Outputs:
- potential: float32 [16, 16384], P('area', 'sec')
The draws below stay inside these ranges and needn't reach their ends.
Inputs may be any that keep to these rules, and one draw needn't show every extreme that they name: `intra_dest`: the 8 target blocks of a source block are distinct; some blocks receive far more synapse blocks than others. `inter_target`: the 2 target areas of a section are distinct; some areas are targeted far more often than others.
All inputs are finite; a program needn't handle non-finite values. No bound on the sum of `spikes` on one device may be relied on, other than what follows from the above.
Results may differ from the reference program's by a relative error of at most 0.000058.
Values sent between devices are 32-bit elements; how exact they have to be, the bound alone decides.
A program may use at most 64 MiB of HBM per device.

```python
import math
import jax
import jax.numpy as jnp
from jax import lax

B = 128
BLK_DEV = 8
FAN = 8
TGT = 2
STEPS = 3
AREAS = 16
SECS = 16
BLOCKS_AREA = 128
NEUR_AREA = 16384


def plant(drawn, own_key, least, high):
    extent = drawn.shape
    index_at = [jax.random.randint(jax.random.fold_in(own_key, axis), (), 0, extent[axis]) for axis in range(len(extent))]
    drawn = drawn.at[tuple(index_at)].set(least)
    longest = extent.index(max(extent))
    index_at[longest] = (index_at[longest] + 1) % extent[longest]
    return drawn.at[tuple(index_at)].set(high)


def levels(own_key, extent, cuts, least, high):
    level, own = 1.0, jax.random.fold_in(own_key, 6)
    for position, parts in cuts:
        draws = jnp.exp(jax.random.uniform(jax.random.fold_in(own, position), (parts,), jnp.float32, least / len(cuts), high / len(cuts)))
        level = level * jnp.repeat(draws, extent[position] // parts).reshape([-1 if axis == position else 1 for axis in range(len(extent))])
    return level


def picks_of(stream_key, rows, number_of, top, lift):
    order = jax.random.permutation(jax.random.fold_in(stream_key, 1), number_of)
    favour = order
    for power in range(3):
        favour = favour * favour // number_of
    favour = favour * lift // number_of
    lots = jax.random.randint(jax.random.fold_in(stream_key, 2), (rows, number_of), 0, 4096) + favour
    holders = jax.random.permutation(jax.random.fold_in(stream_key, 3), rows)[jnp.arange(number_of) % rows]
    lots = jnp.where(jnp.arange(rows)[:, None] == holders[None, :], 1 << 14, lots)
    merit = lots * number_of + jnp.arange(number_of)
    return lax.top_k(merit.astype(jnp.int32), top)[1].astype(jnp.int32)


def gaussian(stream_key, extent, deviation, reach, pieces=(), held_as=jnp.bfloat16):
    drawn = jax.random.normal(stream_key, extent, jnp.float32) * deviation
    if len(pieces) > 0:
        drawn = levels(stream_key, extent, pieces, -0.22, 0.18) * drawn
    return jnp.clip(drawn, min=-reach, max=reach).astype(held_as)


def setup_inputs(seed: int = 0) -> dict:
    arg_keys = jax.random.split(jax.random.key(seed), 8)
    return {
        "spikes": plant((jax.random.randint(arg_keys[0], (AREAS, STEPS, NEUR_AREA), 0, 8) < 1).astype(jnp.int32), jax.random.fold_in(arg_keys[0], 1), 0, 1),
        "intra_weight": gaussian(arg_keys[1], (AREAS, BLOCKS_AREA, FAN, B, B), B ** -0.5, 0.5, ((0, 16), (1, 16)), jnp.float32),
        "intra_dest": picks_of(arg_keys[2], AREAS * BLOCKS_AREA, BLOCKS_AREA, FAN, 1024).reshape((AREAS, BLOCKS_AREA, FAN)),
        "inter_weight": gaussian(arg_keys[3], (AREAS, BLOCKS_AREA, TGT, B, B), B ** -0.5, 0.5, ((0, 16), (1, 16)), jnp.float32),
        "inter_target": picks_of(arg_keys[4], AREAS * SECS, AREAS, TGT, 2048).reshape((AREAS, SECS, TGT)),
        "v_init": jnp.clip(1.0 * jax.random.uniform(arg_keys[5], (AREAS, NEUR_AREA), jnp.float32) ** levels(arg_keys[5], (AREAS, NEUR_AREA), ((0, 16), (1, 16)), -0.2, 0.2), 0.0, 1.0),
        "leak": jnp.clip(jnp.exp(math.log(0.95) - 1.1526795 * jax.random.uniform(arg_keys[6], (AREAS, NEUR_AREA), jnp.float32) ** levels(arg_keys[6], (AREAS, NEUR_AREA), ((0, 16), (1, 16)), -0.2, 0.2)), 0.3, 0.95),
    }


def reference(spikes, intra_weight, intra_dest, inter_weight, inter_target, v_init, leak):
    spiking = spikes.astype(jnp.float32).reshape(AREAS, STEPS, BLOCKS_AREA, B)
    previous = jnp.concatenate([jnp.zeros_like(spiking[:, :1]), spiking[:, :-1]], axis=1)
    intra_part = jnp.einsum("atkn,akfnm->akftm", spiking, intra_weight, precision=lax.Precision.HIGHEST)
    area_index = jnp.arange(AREAS, dtype=jnp.int32)
    intra_keys = (area_index[:, None, None] * BLOCKS_AREA + intra_dest).reshape(-1)
    intra_current = jax.ops.segment_sum(intra_part.reshape(-1, STEPS, B), intra_keys, num_segments=AREAS * BLOCKS_AREA)
    inter_part = jnp.einsum("atkn,akjnm->akjtm", previous, inter_weight, precision=lax.Precision.HIGHEST)
    block_index = jnp.arange(BLOCKS_AREA, dtype=jnp.int32)
    section_of = block_index // BLK_DEV
    targets = inter_target[:, section_of, :]
    inter_keys = (targets * BLOCKS_AREA + block_index[None, :, None]).reshape(-1)
    inter_current = jax.ops.segment_sum(inter_part.reshape(-1, STEPS, B), inter_keys, num_segments=AREAS * BLOCKS_AREA)
    current = (intra_current + inter_current).reshape(AREAS, BLOCKS_AREA, STEPS, B)
    current = current.transpose(0, 2, 1, 3).reshape(AREAS, STEPS, NEUR_AREA)
    drive = spikes.astype(jnp.float32)
    potential = v_init
    for moment in range(STEPS):
        potential = leak * potential * (1.0 - drive[:, moment]) + current[:, moment]
    return potential
```

```python
import functools

import jax
import jax.numpy as jnp
from jax import lax
from jax.experimental import pallas as pl
from jax.experimental.pallas import tpu as pltpu
from jax.sharding import PartitionSpec as P

MESH = pl.DeviceIdType.MESH
F32 = jnp.float32
BF16 = jnp.bfloat16


def split(values):
    high = values.astype(BF16)
    low = (values - high.astype(F32)).astype(BF16)
    return high, low


def kernel(
    areas, secs,
    spikes_ref, dest_ref, target_ref, v_ref, leak_ref, intra_ref, inter_ref,
    out_ref,
    intra_buf, inter_buf, intra_rows, inter_rows, intra_send, inter_send, intra_recv, inter_recv,
    load_sem, load_inter_sem, send_sem, recv_sem,
):
    steps, blocks, width = spikes_ref.shape
    fan = intra_ref.shape[1]
    fan_areas = inter_ref.shape[1]
    me_area = lax.axis_index("area")
    me_sec = lax.axis_index("sec")

    for k in range(blocks):
        pltpu.make_async_copy(intra_ref.at[k], intra_buf.at[k], load_sem.at[k]).start()
    load_inter = pltpu.make_async_copy(inter_ref, inter_buf, load_inter_sem)
    load_inter.start()

    barrier = pltpu.get_barrier_semaphore()
    for i in range(1, secs):
        pl.semaphore_signal(barrier, inc=1, device_id={"sec": lax.rem(me_sec + i, secs)}, device_id_type=MESH)
    for i in range(1, areas):
        pl.semaphore_signal(barrier, inc=1, device_id={"area": lax.rem(me_area + i, areas)}, device_id_type=MESH)

    lane = lax.broadcasted_iota(jnp.int32, (fan, width), 1)
    row = lax.broadcasted_iota(jnp.int32, (fan, width), 0)
    dest = pltpu.roll(dest_ref[...], lax.rem(width - me_sec * blocks, width), 1)
    dest = pltpu.roll(dest, 0, 1, stride=blocks, stride_axis=0)
    dest = jnp.sum(jnp.where(lane // blocks == row, dest, 0), axis=0, keepdims=True)
    half = fan * blocks
    dest = dest + pltpu.roll(dest, half, 1)
    grid_row = lax.broadcasted_iota(jnp.int32, (width, width), 0)
    picker = jnp.where(grid_row == dest, 1.0, 0.0).astype(BF16)

    def spikes_of(k):
        rows = spikes_ref[:, k, :].astype(F32).astype(BF16)
        rows = jnp.concatenate([rows, jnp.zeros((8 - steps, width), BF16)], axis=0)
        return jnp.concatenate([rows, rows], axis=1)

    for k in range(blocks):
        pltpu.make_async_copy(intra_ref.at[k], intra_buf.at[k], load_sem.at[k]).wait()
        lhs = spikes_of(k)
        for f in range(0, fan, 2):
            high, low = split(jnp.concatenate([intra_buf[k, f], intra_buf[k, f + 1]], axis=1))
            part = jnp.dot(lhs, jnp.concatenate([high, low], axis=0), preferred_element_type=F32)
            intra_rows[pl.ds((f * blocks + k) * 8, 8), :] = part[:, :width]
            intra_rows[pl.ds(((f + 1) * blocks + k) * 8, 8), :] = part[:, width:]

    for t in range(steps):
        high, low = split(intra_rows[pl.ds(t, half, stride=8), :])
        grid = jnp.dot(picker, jnp.concatenate([high, low], axis=0), preferred_element_type=F32)
        for p in range(secs):
            intra_send[p, t] = grid[p * blocks:(p + 1) * blocks, :]

    pl.semaphore_wait(barrier, secs - 1 + areas - 1)
    for i in range(1, secs):
        peer = lax.rem(me_sec + i, secs)
        pltpu.make_async_remote_copy(
            src_ref=intra_send.at[peer], dst_ref=intra_recv.at[i - 1],
            send_sem=send_sem.at[0], recv_sem=recv_sem.at[0],
            device_id={"sec": peer}, device_id_type=MESH,
        ).start()

    load_inter.wait()
    for k in range(blocks):
        lhs = spikes_of(k)
        high, low = split(jnp.concatenate([inter_buf[k, 0], inter_buf[k, 1]], axis=1))
        part = jnp.dot(lhs, jnp.concatenate([high, low], axis=0), preferred_element_type=F32)
        for j in range(fan_areas):
            inter_rows[j, pl.ds(k * 8, 8), :] = part[:, j * width:(j + 1) * width]
    for b in range(areas):
        for t in range(steps - 1):
            total = jnp.zeros((blocks, width), F32)
            for j in range(fan_areas):
                chosen = target_ref[j, me_area] == b
                total = jnp.where(chosen, inter_rows[j, pl.ds(t, blocks, stride=8), :], total)
            inter_send[b, t] = total
    for i in range(1, areas):
        peer = lax.rem(me_area + i, areas)
        pltpu.make_async_remote_copy(
            src_ref=inter_send.at[peer], dst_ref=inter_recv.at[i - 1],
            send_sem=send_sem.at[1], recv_sem=recv_sem.at[1],
            device_id={"area": peer}, device_id_type=MESH,
        ).start()

    pltpu.make_async_copy(inter_recv, inter_recv, recv_sem.at[1]).wait()
    inter_current = [inter_send[me_area, t] for t in range(steps - 1)]
    for i in range(areas - 1):
        inter_current = [inter_current[t] + inter_recv[i, t] for t in range(steps - 1)]
    pltpu.make_async_copy(intra_recv, intra_recv, recv_sem.at[0]).wait()
    current = [intra_send[me_sec, t] for t in range(steps)]
    for i in range(secs - 1):
        current = [current[t] + intra_recv[i, t] for t in range(steps)]

    potential = v_ref[...]
    for t in range(steps):
        potential = leak_ref[...] * potential * (1.0 - spikes_ref[t].astype(F32)) + current[t]
        if t > 0:
            potential = potential + inter_current[t - 1]
    out_ref[...] = potential

    pltpu.make_async_copy(inter_recv, inter_recv, send_sem.at[1]).wait()
    pltpu.make_async_copy(intra_recv, intra_recv, send_sem.at[0]).wait()


def body(areas, secs, spikes, intra_weight, intra_dest, inter_weight, inter_target, v_init, leak):
    _, blocks, fan, width, _ = intra_weight.shape
    fan_areas = inter_weight.shape[2]
    steps = spikes.shape[1]
    vmem = pl.BlockSpec(memory_space=pltpu.VMEM)
    smem = pl.BlockSpec(memory_space=pltpu.SMEM)
    anywhere = pl.BlockSpec(memory_space=pl.ANY)
    potential = pl.pallas_call(
        functools.partial(kernel, areas, secs),
        out_shape=jax.ShapeDtypeStruct((blocks, width), F32),
        in_specs=[vmem, vmem, smem, vmem, vmem, anywhere, anywhere],
        out_specs=vmem,
        scratch_shapes=[
            pltpu.VMEM((blocks, fan, width, width), F32),
            pltpu.VMEM((blocks, fan_areas, width, width), F32),
            pltpu.VMEM((fan * blocks * 8, width), F32),
            pltpu.VMEM((fan_areas, blocks * 8, width), F32),
            pltpu.VMEM((secs, steps, blocks, width), F32),
            pltpu.VMEM((areas, steps - 1, blocks, width), F32),
            pltpu.VMEM((secs - 1, steps, blocks, width), F32),
            pltpu.VMEM((areas - 1, steps - 1, blocks, width), F32),
            pltpu.SemaphoreType.DMA((blocks,)),
            pltpu.SemaphoreType.DMA,
            pltpu.SemaphoreType.DMA((2,)),
            pltpu.SemaphoreType.DMA((2,)),
        ],
        compiler_params=pltpu.CompilerParams(
            collective_id=0, has_side_effects=True, vmem_limit_bytes=60 << 20
        ),
    )(
        spikes.reshape(steps, blocks, width),
        intra_dest[0].T,
        inter_target[:, 0, :].T,
        v_init.reshape(blocks, width),
        leak.reshape(blocks, width),
        intra_weight[0],
        inter_weight[0],
    )
    return potential.reshape(1, blocks * width)


def solution(mesh):
    in_specs = (
        P("area", None, "sec"),
        P("area", "sec", None, None, None),
        P("area", None, None),
        P("area", "sec", None, None, None),
        P(None, "sec", None),
        P("area", "sec"),
        P("area", "sec"),
    )
    out_specs = P("area", "sec")
    run = functools.partial(body, mesh.shape["area"], mesh.shape["sec"])
    return jax.shard_map(run, mesh=mesh, in_specs=in_specs, out_specs=out_specs, check_vma=False)
```

```python
import functools

import jax
import jax.numpy as jnp
from jax import lax
from jax.experimental import pallas as pl
from jax.experimental.pallas import tpu as pltpu
from jax.sharding import PartitionSpec as P

MESH = pl.DeviceIdType.MESH
F32 = jnp.float32
BF16 = jnp.bfloat16
SIDE = 4
CORES = 2


def split(values):
    high = values.astype(BF16)
    low = (values - high.astype(F32)).astype(BF16)
    return high, low


def kernel(
    spikes_hbm, dest_hbm, target_hbm, v_hbm, leak_hbm, intra_hbm, inter_hbm,
    out_ref,
    spikes_ref, dest_ref, target_ref, v_ref, leak_ref, intra_buf, inter_buf,
    intra_rows, inter_rows, intra_send, sib_recv, z_send, z_recv,
    x_send, x_recv, y_send, y_recv,
    small_sem, load_sem, send_sem, recv_sem,
):
    steps, blocks, width = spikes_ref.shape
    fan = intra_buf.shape[1]
    fan_areas = inter_buf.shape[1]
    chips = z_send.shape[0]
    later = steps - 1
    me_area = lax.axis_index("area")
    me_sec = lax.axis_index("sec")
    x, y = me_area // SIDE, me_area % SIDE
    z, core = me_sec // CORES, me_sec % CORES

    def at(dx=0, dy=0, dz=0, other=False):
        area = lax.rem(x + dx, SIDE) * SIDE + lax.rem(y + dy, SIDE)
        sec = lax.rem(z + dz, chips) * CORES + (1 - core if other else core)
        return {"area": area, "sec": sec}

    peers = [at(dz=d) for d in sorted(range(1, chips), key=lambda d: -min(d, chips - d))]
    peers += [at(dx=d) for d in (2, 1, 3)] + [at(dy=d) for d in (2, 1, 3)] + [at(other=True)]

    def small(i):
        src = (spikes_hbm, dest_hbm, target_hbm, v_hbm, leak_hbm)[i]
        dst = (spikes_ref, dest_ref, target_ref, v_ref, leak_ref)[i]
        return pltpu.make_async_copy(src, dst, small_sem.at[i])

    def load(k):
        if k == blocks:
            return pltpu.make_async_copy(inter_hbm, inter_buf, load_sem.at[k])
        return pltpu.make_async_copy(intra_hbm.at[k], intra_buf.at[k], load_sem.at[k])

    for i in range(3):
        small(i).start()
    load(blocks).start()
    for k in range(blocks):
        load(k).start()
    barrier = pltpu.get_barrier_semaphore()
    for peer in peers:
        pl.semaphore_signal(barrier, inc=1, device_id=peer, device_id_type=MESH)
    for i in range(3, 5):
        small(i).start()

    for i in range(3):
        small(i).wait()
    lane = lax.broadcasted_iota(jnp.int32, (fan, width), 1)
    row = lax.broadcasted_iota(jnp.int32, (fan, width), 0)
    dest = pltpu.roll(dest_ref[...], lax.rem(width - me_sec * blocks, width), 1)
    dest = pltpu.roll(dest, 0, 1, stride=blocks, stride_axis=0)
    dest = jnp.sum(jnp.where(lane // blocks == row, dest, 0), axis=0, keepdims=True)
    half = fan * blocks
    dest = dest + pltpu.roll(dest, half, 1)
    grid_row = lax.broadcasted_iota(jnp.int32, (width, width), 0)
    picker = jnp.where(grid_row == dest, 1.0, 0.0).astype(BF16)
    target_lane = lax.broadcasted_iota(jnp.int32, target_ref.shape, 1)
    target = jnp.sum(jnp.where(target_lane == me_area, target_ref[...], 0), axis=1, keepdims=True)
    targets = [jnp.broadcast_to(target[j:j + 1], (blocks, width)) for j in range(fan_areas)]

    def spikes_of(k):
        rows = spikes_ref[:, k, :].astype(F32).astype(BF16)
        rows = jnp.concatenate([rows, jnp.zeros((8 - steps, width), BF16)], axis=0)
        return jnp.concatenate([rows, rows], axis=1)

    def products(k, left, right):
        high, low = split(jnp.concatenate([left, right], axis=1))
        rhs = jnp.concatenate([high, low], axis=0)
        part = jnp.dot(spikes_of(k), rhs, preferred_element_type=F32)
        return part[:, :width], part[:, width:]

    load(blocks).wait()
    for k in range(blocks):
        parts = products(k, inter_buf[k, 0], inter_buf[k, 1])
        for j in range(fan_areas):
            inter_rows[j, pl.ds(k * 8, 8), :] = parts[j]
    for t in range(later):
        rows = [inter_rows[j, pl.ds(t, blocks, stride=8), :] for j in range(fan_areas)]
        for b in range(SIDE * SIDE):
            total = jnp.where(targets[0] == b, rows[0], 0.0)
            for j in range(1, fan_areas):
                total = jnp.where(targets[j] == b, rows[j], total)
            x_send[b // SIDE, b % SIDE, t] = total

    for k in range(blocks):
        load(k).wait()
        for f in range(0, fan, 2):
            left, right = products(k, intra_buf[k, f], intra_buf[k, f + 1])
            intra_rows[pl.ds((f * blocks + k) * 8, 8), :] = left
            intra_rows[pl.ds(((f + 1) * blocks + k) * 8, 8), :] = right
    for t in range(steps):
        high, low = split(intra_rows[pl.ds(t, half, stride=8), :])
        grid = jnp.dot(picker, jnp.concatenate([high, low], axis=0), preferred_element_type=F32)
        for p in range(chips * CORES):
            intra_send[p % CORES, p // CORES, t] = grid[p * blocks:(p + 1) * blocks, :]

    def remote(i, src, dst, peer):
        return pltpu.make_async_remote_copy(
            src_ref=src, dst_ref=dst, send_sem=send_sem.at[i], recv_sem=recv_sem.at[i],
            device_id=peer, device_id_type=MESH,
        )

    def wait(sem, i, ref):
        pltpu.make_async_copy(ref, ref, sem.at[i]).wait()

    pl.semaphore_wait(barrier, len(peers))
    remote(0, intra_send.at[1 - core], sib_recv, at(other=True)).start()
    for d in (2, 1, 3):
        remote(1, x_send.at[lax.rem(x + d, SIDE)], x_recv.at[d - 1], at(dx=d)).start()

    wait(recv_sem, 0, sib_recv)
    for p in range(chips):
        for t in range(steps):
            z_send[p, t] = intra_send[core, p, t] + sib_recv[p, t]
    for d in sorted(range(1, chips), key=lambda d: -min(d, chips - d)):
        remote(2, z_send.at[lax.rem(z + d, chips)], z_recv.at[d - 1], at(dz=d)).start()

    wait(recv_sem, 1, x_recv)
    for b in range(SIDE):
        for t in range(later):
            y_send[b, t] = x_send[x, b, t] + x_recv[0, b, t] + x_recv[1, b, t] + x_recv[2, b, t]
    for d in (2, 1, 3):
        remote(3, y_send.at[lax.rem(y + d, SIDE)], y_recv.at[d - 1], at(dy=d)).start()

    for i in range(3, 5):
        small(i).wait()
    wait(recv_sem, 2, z_recv)
    current = [z_send[z, t] for t in range(steps)]
    for i in range(chips - 1):
        current = [current[t] + z_recv[i, t] for t in range(steps)]
    wait(recv_sem, 3, y_recv)
    for t in range(later):
        extra = y_send[y, t]
        for i in range(SIDE - 1):
            extra = extra + y_recv[i, t]
        current[t + 1] = current[t + 1] + extra

    potential = v_ref[...]
    for t in range(steps):
        potential = leak_ref[...] * potential * (1.0 - spikes_ref[t].astype(F32)) + current[t]
    out_ref[...] = potential

    wait(send_sem, 0, sib_recv)
    wait(send_sem, 1, x_recv)
    wait(send_sem, 2, z_recv)
    wait(send_sem, 3, y_recv)


def body(areas, secs, spikes, intra_weight, intra_dest, inter_weight, inter_target, v_init, leak):
    _, blocks, fan, width, _ = intra_weight.shape
    fan_areas = inter_weight.shape[2]
    steps = spikes.shape[1]
    chips = secs // CORES
    assert areas == SIDE * SIDE
    hbm = pl.BlockSpec(memory_space=pl.ANY)
    tile = (blocks, width)
    potential = pl.pallas_call(
        kernel,
        out_shape=jax.ShapeDtypeStruct(tile, F32),
        in_specs=[hbm] * 7,
        out_specs=pl.BlockSpec(memory_space=pltpu.VMEM),
        scratch_shapes=[
            pltpu.VMEM((steps,) + tile, jnp.int32),
            pltpu.VMEM((fan, width), jnp.int32),
            pltpu.VMEM((fan_areas, areas), jnp.int32),
            pltpu.VMEM(tile, F32),
            pltpu.VMEM(tile, F32),
            pltpu.VMEM((blocks, fan, width, width), F32),
            pltpu.VMEM((blocks, fan_areas, width, width), F32),
            pltpu.VMEM((fan * blocks * 8, width), F32),
            pltpu.VMEM((fan_areas, blocks * 8, width), F32),
            pltpu.VMEM((CORES, chips, steps) + tile, F32),
            pltpu.VMEM((chips, steps) + tile, F32),
            pltpu.VMEM((chips, steps) + tile, F32),
            pltpu.VMEM((chips - 1, steps) + tile, F32),
            pltpu.VMEM((SIDE, SIDE, steps - 1) + tile, F32),
            pltpu.VMEM((SIDE - 1, SIDE, steps - 1) + tile, F32),
            pltpu.VMEM((SIDE, steps - 1) + tile, F32),
            pltpu.VMEM((SIDE - 1, steps - 1) + tile, F32),
            pltpu.SemaphoreType.DMA((5,)),
            pltpu.SemaphoreType.DMA((blocks + 1,)),
            pltpu.SemaphoreType.DMA((4,)),
            pltpu.SemaphoreType.DMA((4,)),
        ],
        compiler_params=pltpu.CompilerParams(
            collective_id=0, has_side_effects=True, vmem_limit_bytes=60 << 20
        ),
    )(
        spikes.reshape((steps,) + tile),
        intra_dest[0].T,
        inter_target[:, 0, :].T,
        v_init.reshape(tile),
        leak.reshape(tile),
        intra_weight[0],
        inter_weight[0],
    )
    return potential.reshape(1, blocks * width)


def solution(mesh):
    in_specs = (
        P("area", None, "sec"),
        P("area", "sec", None, None, None),
        P("area", None, None),
        P("area", "sec", None, None, None),
        P(None, "sec", None),
        P("area", "sec"),
        P("area", "sec"),
    )
    out_specs = P("area", "sec")
    run = functools.partial(body, mesh.shape["area"], mesh.shape["sec"])
    return jax.shard_map(run, mesh=mesh, in_specs=in_specs, out_specs=out_specs, check_vma=False)
```

```python
import functools

import jax
import jax.numpy as jnp
from jax import lax
from jax.experimental import pallas as pl
from jax.experimental.pallas import tpu as pltpu
from jax.sharding import PartitionSpec as P

MESH = pl.DeviceIdType.MESH
F32 = jnp.float32
BF16 = jnp.bfloat16
SIDE = 4
CORES = 2


def split(values):
    high = values.astype(BF16)
    low = (values - high.astype(F32)).astype(BF16)
    return high, low


def kernel(
    spikes_hbm, dest_hbm, target_hbm, v_hbm, leak_hbm, intra_hbm, inter_hbm,
    held_ref, last_ref,
    spikes_ref, dest_ref, target_ref, v_ref, leak_ref, intra_buf, inter_buf,
    intra_rows, inter_rows, intra_send, sib_recv, z_send, z_recv,
    x_send, x_recv, y_send, y_recv,
    small_sem, load_sem, send_sem, recv_sem, ready_sem,
):
    steps, blocks, width = spikes_ref.shape
    fan = intra_buf.shape[1]
    fan_areas = inter_buf.shape[1]
    chips = z_send.shape[0]
    later = steps - 1
    me_area = lax.axis_index("area")
    me_sec = lax.axis_index("sec")
    x, y = me_area // SIDE, me_area % SIDE
    z, core = me_sec // CORES, me_sec % CORES

    def at(dx=0, dy=0, dz=0, other=False):
        area = lax.rem(x + dx, SIDE) * SIDE + lax.rem(y + dy, SIDE)
        sec = lax.rem(z + dz, chips) * CORES + (1 - core if other else core)
        return {"area": area, "sec": sec}

    far_z = sorted(range(1, chips), key=lambda d: -min(d, chips - d))
    axes = (
        (z, chips, far_z, lambda d: at(dz=d)),
        (x, SIDE, (2, 1, 3), lambda d: at(dx=d)),
        (y, SIDE, (2, 1, 3), lambda d: at(dy=d)),
    )

    def partners(axis, after, act):
        place, length, distances, peer = axes[axis]
        for d in distances:
            follows = place + d < length

            @pl.when(follows if after else jnp.logical_not(follows))
            def _():
                act(d, peer(d))

    def small(i):
        src = (spikes_hbm, dest_hbm, target_hbm, v_hbm, leak_hbm)[i]
        dst = (spikes_ref, dest_ref, target_ref, v_ref, leak_ref)[i]
        return pltpu.make_async_copy(src, dst, small_sem.at[i])

    def load(k):
        if k == blocks:
            return pltpu.make_async_copy(inter_hbm, inter_buf, load_sem.at[k])
        return pltpu.make_async_copy(intra_hbm.at[k], intra_buf.at[k], load_sem.at[k])

    def remote(i, src, dst, peer):
        return pltpu.make_async_remote_copy(
            src_ref=src, dst_ref=dst, send_sem=send_sem.at[i], recv_sem=recv_sem.at[i],
            device_id=peer, device_id_type=MESH,
        )

    def wait(sem, i, ref):
        pltpu.make_async_copy(ref, ref, sem.at[i]).wait()

    def send_x(d, peer):
        remote(1, x_send.at[lax.rem(x + d, SIDE)], x_recv.at[d - 1], peer).start()

    def send_z(d, peer):
        remote(2, z_send.at[lax.rem(z + d, chips)], z_recv.at[d - 1], peer).start()

    def send_y(d, peer):
        remote(3, y_send.at[lax.rem(y + d, SIDE)], y_recv.at[d - 1], peer).start()

    def entered(axis):
        place, length, _, _ = axes[axis]

        @pl.when(place < length - 1)
        def _():
            pl.semaphore_wait(ready_sem.at[axis], length - 1 - place)

    for i in range(3):
        small(i).start()
    load(blocks).start()
    for k in range(blocks):
        load(k).start()
    barrier = pltpu.get_barrier_semaphore()
    for axis in range(3):
        partners(axis, True, lambda d, peer: pl.semaphore_signal(barrier, inc=1, device_id=peer, device_id_type=MESH))
    pl.semaphore_signal(barrier, inc=1, device_id=at(other=True), device_id_type=MESH)
    for i in range(3, 5):
        small(i).start()

    for i in range(3):
        small(i).wait()
    lane = lax.broadcasted_iota(jnp.int32, (fan, width), 1)
    row = lax.broadcasted_iota(jnp.int32, (fan, width), 0)
    dest = pltpu.roll(dest_ref[...], lax.rem(width - me_sec * blocks, width), 1)
    dest = pltpu.roll(dest, 0, 1, stride=blocks, stride_axis=0)
    dest = jnp.sum(jnp.where(lane // blocks == row, dest, 0), axis=0, keepdims=True)
    half = fan * blocks
    dest = dest + pltpu.roll(dest, half, 1)
    grid_row = lax.broadcasted_iota(jnp.int32, (width, width), 0)
    picker = jnp.where(grid_row == dest, 1.0, 0.0).astype(BF16)
    target_lane = lax.broadcasted_iota(jnp.int32, target_ref.shape, 1)
    target = jnp.sum(jnp.where(target_lane == me_area, target_ref[...], 0), axis=1, keepdims=True)
    targets = [jnp.broadcast_to(target[j:j + 1], (blocks, width)) for j in range(fan_areas)]

    def spikes_of(k):
        rows = spikes_ref[:, k, :].astype(F32).astype(BF16)
        rows = jnp.concatenate([rows, jnp.zeros((8 - steps, width), BF16)], axis=0)
        return jnp.concatenate([rows, rows], axis=1)

    def products(k, left, right):
        high, low = split(jnp.concatenate([left, right], axis=1))
        rhs = jnp.concatenate([high, low], axis=0)
        part = jnp.dot(spikes_of(k), rhs, preferred_element_type=F32)
        return part[:, :width], part[:, width:]

    pl.semaphore_wait(barrier, 1 + x + y + z)
    for axis in range(3):
        ready = ready_sem.at[axis]
        partners(axis, False, lambda d, peer: pl.semaphore_signal(ready, inc=1, device_id=peer, device_id_type=MESH))

    for k in [blocks] + list(range(blocks // 2)):
        load(k).wait()
    for k in range(blocks):
        parts = products(k, inter_buf[k, 0], inter_buf[k, 1])
        for j in range(fan_areas):
            inter_rows[j, pl.ds(k * 8, 8), :] = parts[j]
    for t in range(later):
        rows = [inter_rows[j, pl.ds(t, blocks, stride=8), :] for j in range(fan_areas)]
        for b in range(SIDE * SIDE):
            total = jnp.where(targets[0] == b, rows[0], 0.0)
            for j in range(1, fan_areas):
                total = jnp.where(targets[j] == b, rows[j], total)
            x_send[b // SIDE, b % SIDE, t] = total

    def intra(k):
        for f in range(0, fan, 2):
            left, right = products(k, intra_buf[k, f], intra_buf[k, f + 1])
            intra_rows[pl.ds((f * blocks + k) * 8, 8), :] = left
            intra_rows[pl.ds(((f + 1) * blocks + k) * 8, 8), :] = right

    for k in range(blocks // 2):
        intra(k)
    partners(1, False, send_x)


    for k in range(blocks // 2, blocks):
        load(k).wait()
    for k in range(blocks // 2, blocks):
        intra(k)
    for t in range(steps):
        high, low = split(intra_rows[pl.ds(t, half, stride=8), :])
        grid = jnp.dot(picker, jnp.concatenate([high, low], axis=0), preferred_element_type=F32)
        for p in range(chips * CORES):
            intra_send[p % CORES, p // CORES, t] = grid[p * blocks:(p + 1) * blocks, :]

    remote(0, intra_send.at[1 - core], sib_recv, at(other=True)).start()

    wait(recv_sem, 0, sib_recv)
    for p in range(chips):
        for t in range(steps):
            z_send[p, t] = intra_send[core, p, t] + sib_recv[p, t]
    partners(0, False, send_z)
    entered(1)
    partners(1, True, send_x)

    wait(recv_sem, 1, x_recv)
    for b in range(SIDE):
        for t in range(later):
            y_send[b, t] = x_send[x, b, t] + x_recv[0, b, t] + x_recv[1, b, t] + x_recv[2, b, t]
    partners(2, False, send_y)
    entered(0)
    partners(0, True, send_z)
    entered(2)
    partners(2, True, send_y)

    for i in range(3, 5):
        small(i).wait()
    wait(recv_sem, 2, z_recv)
    current = [z_send[z, t] for t in range(steps)]
    for i in range(chips - 1):
        current = [current[t] + z_recv[i, t] for t in range(steps)]
    wait(recv_sem, 3, y_recv)
    for t in range(later):
        extra = y_send[y, t]
        for i in range(SIDE - 1):
            extra = extra + y_recv[i, t]
        current[t + 1] = current[t + 1] + extra

    potential = v_ref[...]
    for t in range(later):
        potential = leak_ref[...] * potential * (1.0 - spikes_ref[t].astype(F32)) + current[t]
    held_ref[...] = leak_ref[...] * potential * (1.0 - spikes_ref[later].astype(F32))
    last_ref[...] = current[later]

    wait(send_sem, 0, sib_recv)
    wait(send_sem, 1, x_recv)
    wait(send_sem, 2, z_recv)
    wait(send_sem, 3, y_recv)


def body(areas, secs, spikes, intra_weight, intra_dest, inter_weight, inter_target, v_init, leak):
    _, blocks, fan, width, _ = intra_weight.shape
    fan_areas = inter_weight.shape[2]
    steps = spikes.shape[1]
    chips = secs // CORES
    assert areas == SIDE * SIDE
    hbm = pl.BlockSpec(memory_space=pltpu.HBM)
    tile = (blocks, width)
    held, last = pl.pallas_call(
        kernel,
        out_shape=[jax.ShapeDtypeStruct(tile, F32)] * 2,
        in_specs=[hbm] * 7,
        out_specs=[pl.BlockSpec(memory_space=pltpu.VMEM)] * 2,
        scratch_shapes=[
            pltpu.VMEM((steps,) + tile, jnp.int32),
            pltpu.VMEM((fan, width), jnp.int32),
            pltpu.VMEM((fan_areas, areas), jnp.int32),
            pltpu.VMEM(tile, F32),
            pltpu.VMEM(tile, F32),
            pltpu.VMEM((blocks, fan, width, width), F32),
            pltpu.VMEM((blocks, fan_areas, width, width), F32),
            pltpu.VMEM((fan * blocks * 8, width), F32),
            pltpu.VMEM((fan_areas, blocks * 8, width), F32),
            pltpu.VMEM((CORES, chips, steps) + tile, F32),
            pltpu.VMEM((chips, steps) + tile, F32),
            pltpu.VMEM((chips, steps) + tile, F32),
            pltpu.VMEM((chips - 1, steps) + tile, F32),
            pltpu.VMEM((SIDE, SIDE, steps - 1) + tile, F32),
            pltpu.VMEM((SIDE - 1, SIDE, steps - 1) + tile, F32),
            pltpu.VMEM((SIDE, steps - 1) + tile, F32),
            pltpu.VMEM((SIDE - 1, steps - 1) + tile, F32),
            pltpu.SemaphoreType.DMA((5,)),
            pltpu.SemaphoreType.DMA((blocks + 1,)),
            pltpu.SemaphoreType.DMA((4,)),
            pltpu.SemaphoreType.DMA((4,)),
            pltpu.SemaphoreType.REGULAR((3,)),
        ],
        compiler_params=pltpu.CompilerParams(
            collective_id=0, has_side_effects=True, vmem_limit_bytes=16 << 20
        ),
    )(*(
        pltpu.with_memory_space_constraint(operand, pltpu.HBM)
        for operand in (
            spikes.reshape((steps,) + tile),
            intra_dest[0].T,
            inter_target[:, 0, :].T,
            v_init.reshape(tile),
            leak.reshape(tile),
            intra_weight[0],
            inter_weight[0],
        )
    ))
    return (held + last).reshape(1, blocks * width)


def solution(mesh):
    in_specs = (
        P("area", None, "sec"),
        P("area", "sec", None, None, None),
        P("area", None, None),
        P("area", "sec", None, None, None),
        P(None, "sec", None),
        P("area", "sec"),
        P("area", "sec"),
    )
    out_specs = P("area", "sec")
    run = functools.partial(body, mesh.shape["area"], mesh.shape["sec"])
    return jax.shard_map(run, mesh=mesh, in_specs=in_specs, out_specs=out_specs, check_vma=False)
```

```python
import functools

import jax
import jax.numpy as jnp
from jax import lax
from jax.experimental import pallas as pl
from jax.experimental.pallas import tpu as pltpu
from jax.sharding import PartitionSpec as P

MESH = pl.DeviceIdType.MESH
F32 = jnp.float32
BF16 = jnp.bfloat16
SIDE = 4
HALVES = 2
CORES = 2


def split(values):
    high = values.astype(BF16)
    low = (values - high.astype(F32)).astype(BF16)
    return high, low


def kernel(
    spikes_hbm, dest_hbm, target_hbm, v_hbm, leak_hbm, intra_hbm, inter_hbm,
    held_ref, last_ref,
    spikes_ref, dest_ref, target_ref, v_ref, leak_ref, intra_buf, inter_buf,
    intra_rows, inter_rows, intra_send, sib_recv, z_send, z_recv,
    x_send, x_recv, y_send, y_recv,
    small_sem, load_sem, send_sem, recv_sem, ready_sem,
):
    steps, blocks, width = spikes_ref.shape
    fan = intra_buf.shape[1]
    fan_areas = inter_buf.shape[1]
    chips = z_send.shape[0]
    later = steps - 1
    me_area = lax.axis_index("area")
    me_sec = lax.axis_index("sec")
    x, y = me_area // SIDE, me_area % SIDE
    z, core = me_sec // CORES, me_sec % CORES

    def at(dx=0, dy=0, dz=0, other=False):
        area = lax.rem(x + dx, SIDE) * SIDE + lax.rem(y + dy, SIDE)
        sec = lax.rem(z + dz, chips) * CORES + (1 - core if other else core)
        return {"area": area, "sec": sec}

    far_z = sorted(range(1, chips), key=lambda d: -min(d, chips - d))
    axes = (
        (z, chips, far_z, lambda d: at(dz=d)),
        (x, SIDE, (2, 1, 3), lambda d: at(dx=d)),
        (y, SIDE, (2, 1, 3), lambda d: at(dy=d)),
    )

    def partners(axis, after, act):
        place, length, distances, peer = axes[axis]
        for d in distances if after else sorted(distances):
            follows = place + d < length

            @pl.when(follows if after else jnp.logical_not(follows))
            def _():
                act(d, peer(d))

    def small(i):
        src = (spikes_hbm, dest_hbm, target_hbm, v_hbm, leak_hbm)[i]
        dst = (spikes_ref, dest_ref, target_ref, v_ref, leak_ref)[i]
        return pltpu.make_async_copy(src, dst, small_sem.at[i])

    def load(k):
        if k == HALVES:
            return pltpu.make_async_copy(inter_hbm, inter_buf, load_sem.at[k])
        half = pl.ds(k * (blocks // HALVES), blocks // HALVES)
        return pltpu.make_async_copy(intra_hbm.at[half], intra_buf.at[half], load_sem.at[k])

    def remote(i, src, dst, peer):
        return pltpu.make_async_remote_copy(
            src_ref=src, dst_ref=dst, send_sem=send_sem.at[i], recv_sem=recv_sem.at[i],
            device_id=peer, device_id_type=MESH,
        )

    def wait(sem, i, ref):
        pltpu.make_async_copy(ref, ref, sem.at[i]).wait()

    def send_x(d, peer):
        remote(1, x_send.at[lax.rem(x + d, SIDE)], x_recv.at[d - 1], peer).start()

    def send_z(d, peer):
        remote(2, z_send.at[lax.rem(z + d, chips)], z_recv.at[d - 1], peer).start()

    def send_y(d, peer):
        remote(3, y_send.at[lax.rem(y + d, SIDE)], y_recv.at[d - 1], peer).start()

    def entered(axis):
        place, length, _, _ = axes[axis]

        @pl.when(place < length - 1)
        def _():
            pl.semaphore_wait(ready_sem.at[axis], length - 1 - place)

    for k in (HALVES, 0, 1):
        load(k).start()
    for i in range(3):
        small(i).start()
    barrier = pltpu.get_barrier_semaphore()
    for axis in range(3):
        partners(axis, True, lambda d, peer: pl.semaphore_signal(barrier, inc=1, device_id=peer, device_id_type=MESH))
    pl.semaphore_signal(barrier, inc=1, device_id=at(other=True), device_id_type=MESH)
    for i in range(3, 5):
        small(i).start()

    pl.semaphore_wait(barrier, 1 + x + y + z)
    for axis in range(3):
        ready = ready_sem.at[axis]
        partners(axis, False, lambda d, peer: pl.semaphore_signal(ready, inc=1, device_id=peer, device_id_type=MESH))

    for i in range(3):
        small(i).wait()
    lane = lax.broadcasted_iota(jnp.int32, (fan, width), 1)
    row = lax.broadcasted_iota(jnp.int32, (fan, width), 0)
    dest = pltpu.roll(dest_ref[...], lax.rem(width - me_sec * blocks, width), 1)
    dest = pltpu.roll(dest, 0, 1, stride=blocks, stride_axis=0)
    dest = jnp.sum(jnp.where(lane // blocks == row, dest, 0), axis=0, keepdims=True)
    half = fan * blocks
    dest = dest + pltpu.roll(dest, half, 1)
    grid_row = lax.broadcasted_iota(jnp.int32, (width, width), 0)
    picker = jnp.where(grid_row == dest, 1.0, 0.0).astype(BF16)
    target_lane = lax.broadcasted_iota(jnp.int32, target_ref.shape, 1)
    target = jnp.sum(jnp.where(target_lane == me_area, target_ref[...], 0), axis=1, keepdims=True)
    targets = [jnp.broadcast_to(target[j:j + 1], (blocks, width)) for j in range(fan_areas)]

    def spikes_of(k):
        rows = spikes_ref[:, k, :].astype(F32).astype(BF16)
        rows = jnp.concatenate([rows, jnp.zeros((8 - steps, width), BF16)], axis=0)
        return jnp.concatenate([rows, rows], axis=1)

    def products(k, left, right):
        high, low = split(jnp.concatenate([left, right], axis=1))
        rhs = jnp.concatenate([high, low], axis=0)
        part = jnp.dot(spikes_of(k), rhs, preferred_element_type=F32)
        return part[:, :width], part[:, width:]

    load(HALVES).wait()
    load(0).wait()
    for k in range(blocks):
        parts = products(k, inter_buf[k, 0], inter_buf[k, 1])
        for j in range(fan_areas):
            inter_rows[j, pl.ds(k * 8, 8), :] = parts[j]
    for t in range(later):
        rows = [inter_rows[j, pl.ds(t, blocks, stride=8), :] for j in range(fan_areas)]
        for b in range(SIDE * SIDE):
            total = jnp.where(targets[0] == b, rows[0], 0.0)
            for j in range(1, fan_areas):
                total = jnp.where(targets[j] == b, rows[j], total)
            x_send[b // SIDE, b % SIDE, t] = total

    def intra(k):
        for f in range(0, fan, 2):
            left, right = products(k, intra_buf[k, f], intra_buf[k, f + 1])
            intra_rows[pl.ds((f * blocks + k) * 8, 8), :] = left
            intra_rows[pl.ds(((f + 1) * blocks + k) * 8, 8), :] = right

    for k in range(blocks // 2):
        intra(k)

    partners(1, False, send_x)
    load(1).wait()
    for k in range(blocks // 2, blocks):
        intra(k)
    for t in range(steps):
        high, low = split(intra_rows[pl.ds(t, half, stride=8), :])
        grid = jnp.dot(picker, jnp.concatenate([high, low], axis=0), preferred_element_type=F32)
        for p in range(chips * CORES):
            intra_send[p % CORES, p // CORES, t] = grid[p * blocks:(p + 1) * blocks, :]

    remote(0, intra_send.at[1 - core], sib_recv, at(other=True)).start()


    wait(recv_sem, 0, sib_recv)
    for p in range(chips):
        for t in range(steps):
            z_send[p, t] = intra_send[core, p, t] + sib_recv[p, t]
    partners(0, False, send_z)
    entered(1)
    partners(1, True, send_x)

    wait(recv_sem, 1, x_recv)
    for b in range(SIDE):
        for t in range(later):
            y_send[b, t] = x_send[x, b, t] + x_recv[0, b, t] + x_recv[1, b, t] + x_recv[2, b, t]
    partners(2, False, send_y)
    entered(0)
    partners(0, True, send_z)
    entered(2)
    partners(2, True, send_y)

    for i in range(3, 5):
        small(i).wait()
    wait(recv_sem, 3, y_recv)
    current = [z_send[z, t] for t in range(steps)]
    for t in range(later):
        extra = y_send[y, t]
        for i in range(SIDE - 1):
            extra = extra + y_recv[i, t]
        current[t + 1] = current[t + 1] + extra
    wait(recv_sem, 2, z_recv)
    for i in range(chips - 1):
        current = [current[t] + z_recv[i, t] for t in range(steps)]

    potential = v_ref[...]
    for t in range(later):
        potential = leak_ref[...] * potential * (1.0 - spikes_ref[t].astype(F32)) + current[t]
    held_ref[...] = leak_ref[...] * potential * (1.0 - spikes_ref[later].astype(F32))
    last_ref[...] = current[later]

    wait(send_sem, 0, sib_recv)
    wait(send_sem, 1, x_recv)
    wait(send_sem, 2, z_recv)
    wait(send_sem, 3, y_recv)


def body(areas, secs, spikes, intra_weight, intra_dest, inter_weight, inter_target, v_init, leak):
    _, blocks, fan, width, _ = intra_weight.shape
    fan_areas = inter_weight.shape[2]
    steps = spikes.shape[1]
    chips = secs // CORES
    assert areas == SIDE * SIDE
    hbm = pl.BlockSpec(memory_space=pltpu.HBM)
    tile = (blocks, width)
    held, last = pl.pallas_call(
        kernel,
        out_shape=[jax.ShapeDtypeStruct(tile, F32)] * 2,
        in_specs=[hbm] * 7,
        out_specs=[pl.BlockSpec(memory_space=pltpu.VMEM)] * 2,
        scratch_shapes=[
            pltpu.VMEM((steps,) + tile, jnp.int32),
            pltpu.VMEM((fan, width), jnp.int32),
            pltpu.VMEM((fan_areas, areas), jnp.int32),
            pltpu.VMEM(tile, F32),
            pltpu.VMEM(tile, F32),
            pltpu.VMEM((blocks, fan, width, width), F32),
            pltpu.VMEM((blocks, fan_areas, width, width), F32),
            pltpu.VMEM((fan * blocks * 8, width), F32),
            pltpu.VMEM((fan_areas, blocks * 8, width), F32),
            pltpu.VMEM((CORES, chips, steps) + tile, F32),
            pltpu.VMEM((chips, steps) + tile, F32),
            pltpu.VMEM((chips, steps) + tile, F32),
            pltpu.VMEM((chips - 1, steps) + tile, F32),
            pltpu.VMEM((SIDE, SIDE, steps - 1) + tile, F32),
            pltpu.VMEM((SIDE - 1, SIDE, steps - 1) + tile, F32),
            pltpu.VMEM((SIDE, steps - 1) + tile, F32),
            pltpu.VMEM((SIDE - 1, steps - 1) + tile, F32),
            pltpu.SemaphoreType.DMA((5,)),
            pltpu.SemaphoreType.DMA((HALVES + 1,)),
            pltpu.SemaphoreType.DMA((4,)),
            pltpu.SemaphoreType.DMA((4,)),
            pltpu.SemaphoreType.REGULAR((3,)),
        ],
        compiler_params=pltpu.CompilerParams(
            collective_id=0, has_side_effects=True, vmem_limit_bytes=16 << 20
        ),
    )(*(
        pltpu.with_memory_space_constraint(operand, pltpu.HBM)
        for operand in (
            spikes.reshape((steps,) + tile),
            intra_dest[0].T,
            inter_target[:, 0, :].T,
            v_init.reshape(tile),
            leak.reshape(tile),
            intra_weight[0],
            inter_weight[0],
        )
    ))
    return (held + last).reshape(1, blocks * width)


def solution(mesh):
    in_specs = (
        P("area", None, "sec"),
        P("area", "sec", None, None, None),
        P("area", None, None),
        P("area", "sec", None, None, None),
        P(None, "sec", None),
        P("area", "sec"),
        P("area", "sec"),
    )
    out_specs = P("area", "sec")
    run = functools.partial(body, mesh.shape["area"], mesh.shape["sec"])
    return jax.shard_map(run, mesh=mesh, in_specs=in_specs, out_specs=out_specs, check_vma=False)
```

```python
import functools

import jax
import jax.numpy as jnp
from jax import lax
from jax.experimental import pallas as pl
from jax.experimental.pallas import tpu as pltpu
from jax.sharding import PartitionSpec as P

MESH = pl.DeviceIdType.MESH
F32 = jnp.float32
BF16 = jnp.bfloat16
SIDE = 4
HALVES = 2
CORES = 2


def split(values):
    high = values.astype(BF16)
    low = (values - high.astype(F32)).astype(BF16)
    return high, low


def kernel(
    spikes_hbm, dest_hbm, target_hbm, v_hbm, leak_hbm, intra_hbm, inter_hbm,
    held_ref, last_ref,
    spikes_ref, dest_ref, target_ref, v_ref, leak_ref, intra_buf, inter_buf,
    intra_rows, inter_rows, intra_send, sib_recv, z_send, z_recv,
    x_send, x_recv, y_send, y_recv,
    small_sem, load_sem, send_sem, recv_sem, ready_sem,
):
    steps, blocks, width = spikes_ref.shape
    fan = intra_buf.shape[1]
    fan_areas = inter_buf.shape[1]
    chips = z_send.shape[0]
    later = steps - 1
    me_area = lax.axis_index("area")
    me_sec = lax.axis_index("sec")
    x, y = me_area // SIDE, me_area % SIDE
    z, core = me_sec // CORES, me_sec % CORES

    def at(dx=0, dy=0, dz=0, other=False):
        area = lax.rem(x + dx, SIDE) * SIDE + lax.rem(y + dy, SIDE)
        sec = lax.rem(z + dz, chips) * CORES + (1 - core if other else core)
        return {"area": area, "sec": sec}

    late = chips // 2
    is_late = z >= late

    far_z = sorted(range(1, chips), key=lambda d: -min(d, chips - d))
    axes = (
        (z, chips, far_z, lambda d: at(dz=d)),
        (x, SIDE, (2, 1, 3), lambda d: at(dx=d)),
        (y, SIDE, (2, 1, 3), lambda d: at(dy=d)),
    )

    def partners(axis, after, act):
        place, length, distances, peer = axes[axis]
        for d in distances if after else sorted(distances):
            follows = place + d < length

            @pl.when(follows if after else jnp.logical_not(follows))
            def _():
                act(d, peer(d))

    def small(i):
        src = (spikes_hbm, dest_hbm, target_hbm, v_hbm, leak_hbm)[i]
        dst = (spikes_ref, dest_ref, target_ref, v_ref, leak_ref)[i]
        return pltpu.make_async_copy(src, dst, small_sem.at[i])

    def load(k):
        if k == HALVES:
            return pltpu.make_async_copy(inter_hbm, inter_buf, load_sem.at[k])
        half = pl.ds(k * (blocks // HALVES), blocks // HALVES)
        return pltpu.make_async_copy(intra_hbm.at[half], intra_buf.at[half], load_sem.at[k])

    def remote(i, src, dst, peer):
        return pltpu.make_async_remote_copy(
            src_ref=src, dst_ref=dst, send_sem=send_sem.at[i], recv_sem=recv_sem.at[i],
            device_id=peer, device_id_type=MESH,
        )

    def wait(sem, i, ref):
        pltpu.make_async_copy(ref, ref, sem.at[i]).wait()

    def send_x(d, peer):
        remote(1, x_send.at[lax.rem(x + d, SIDE)], x_recv.at[d - 1], peer).start()

    def send_z(d, peer):
        remote(2, z_send.at[lax.rem(z + d, chips)], z_recv.at[d - 1], peer).start()

    def send_y(d, peer):
        remote(3, y_send.at[lax.rem(y + d, SIDE)], y_recv.at[d - 1], peer).start()

    def entered(axis):
        place, length, _, _ = axes[axis]

        @pl.when(place < length - 1)
        def _():
            pl.semaphore_wait(ready_sem.at[axis], length - 1 - place)

    for k in range(HALVES + 1):
        load(k).start()
    for i in range(3):
        small(i).start()
    barrier = pltpu.get_barrier_semaphore()
    for axis in range(3):
        partners(axis, True, lambda d, peer: pl.semaphore_signal(barrier, inc=1, device_id=peer, device_id_type=MESH))
    pl.semaphore_signal(barrier, inc=1, device_id=at(other=True), device_id_type=MESH)

    @pl.when(z == 0)
    def _():
        for d in range(late, chips):
            pl.semaphore_signal(barrier, inc=1, device_id=at(dz=d, other=True), device_id_type=MESH)

    for i in range(3, 5):
        small(i).start()

    pl.semaphore_wait(barrier, 1 + x + y + z + z // late)
    for axis in range(3):
        ready = ready_sem.at[axis]
        partners(axis, False, lambda d, peer: pl.semaphore_signal(ready, inc=1, device_id=peer, device_id_type=MESH))

    for i in range(3):
        small(i).wait()
    lane = lax.broadcasted_iota(jnp.int32, (fan, width), 1)
    row = lax.broadcasted_iota(jnp.int32, (fan, width), 0)
    dest = pltpu.roll(dest_ref[...], lax.rem(width - me_sec * blocks, width), 1)
    dest = pltpu.roll(dest, 0, 1, stride=blocks, stride_axis=0)
    dest = jnp.sum(jnp.where(lane // blocks == row, dest, 0), axis=0, keepdims=True)
    half = fan * blocks
    dest = dest + pltpu.roll(dest, half, 1)
    grid_row = lax.broadcasted_iota(jnp.int32, (width, width), 0)
    picker = jnp.where(grid_row == dest, 1.0, 0.0).astype(BF16)
    target_lane = lax.broadcasted_iota(jnp.int32, target_ref.shape, 1)
    target = jnp.sum(jnp.where(target_lane == me_area, target_ref[...], 0), axis=1, keepdims=True)
    targets = [jnp.broadcast_to(target[j:j + 1], (blocks, width)) for j in range(fan_areas)]

    def spikes_of(k):
        rows = spikes_ref[:, k, :].astype(F32).astype(BF16)
        rows = jnp.concatenate([rows, jnp.zeros((8 - steps, width), BF16)], axis=0)
        return jnp.concatenate([rows, rows], axis=1)

    def products(k, left, right):
        high, low = split(jnp.concatenate([left, right], axis=1))
        rhs = jnp.concatenate([high, low], axis=0)
        part = jnp.dot(spikes_of(k), rhs, preferred_element_type=F32)
        return part[:, :width], part[:, width:]

    def intra(k):
        for f in range(0, fan, 2):
            left, right = products(k, intra_buf[k, f], intra_buf[k, f + 1])
            intra_rows[pl.ds((f * blocks + k) * 8, 8), :] = left
            intra_rows[pl.ds(((f + 1) * blocks + k) * 8, 8), :] = right

    load(0).wait()
    for k in range(blocks // 2):
        intra(k)

    load(1).wait()
    for k in range(blocks // 2, blocks):
        intra(k)
    for t in range(steps):
        high, low = split(intra_rows[pl.ds(t, half, stride=8), :])
        grid = jnp.dot(picker, jnp.concatenate([high, low], axis=0), preferred_element_type=F32)
        for p in range(chips * CORES):
            intra_send[p % CORES, p // CORES, t] = grid[p * blocks:(p + 1) * blocks, :]


    @pl.when(is_late)
    def _():
        back = chips - z
        remote(2, intra_send.at[core, 0], z_recv.at[back - 1], at(dz=back)).start()
        remote(2, intra_send.at[1 - core, 0], z_recv.at[chips - 2 + back], at(dz=back, other=True)).start()

    remote(0, intra_send.at[1 - core], sib_recv, at(other=True)).start()

    load(HALVES).wait()
    for k in range(blocks):
        parts = products(k, inter_buf[k, 0], inter_buf[k, 1])
        for j in range(fan_areas):
            inter_rows[j, pl.ds(k * 8, 8), :] = parts[j]
    for t in range(later):
        rows = [inter_rows[j, pl.ds(t, blocks, stride=8), :] for j in range(fan_areas)]
        for b in range(SIDE * SIDE):
            total = jnp.where(targets[0] == b, rows[0], 0.0)
            for j in range(1, fan_areas):
                total = jnp.where(targets[j] == b, rows[j], total)
            x_send[b // SIDE, b % SIDE, t] = total

    partners(1, False, send_x)

    wait(recv_sem, 0, sib_recv)
    for p in range(chips):
        for t in range(steps):
            z_send[p, t] = intra_send[core, p, t] + sib_recv[p, t]
    def send_z_summed(d, peer):
        @pl.when(jnp.logical_not(jnp.logical_and(is_late, z + d == chips)))
        def _():
            send_z(d, peer)

    partners(0, False, send_z_summed)
    entered(1)
    partners(1, True, send_x)

    wait(recv_sem, 1, x_recv)
    for b in range(SIDE):
        for t in range(later):
            y_send[b, t] = x_send[x, b, t] + x_recv[0, b, t] + x_recv[1, b, t] + x_recv[2, b, t]
    partners(2, False, send_y)
    entered(0)
    partners(0, True, send_z)
    entered(2)
    partners(2, True, send_y)

    for i in range(3, 5):
        small(i).wait()
    wait(recv_sem, 3, y_recv)
    current = [z_send[z, t] for t in range(steps)]
    for t in range(later):
        extra = y_send[y, t]
        for i in range(SIDE - 1):
            extra = extra + y_recv[i, t]
        current[t + 1] = current[t + 1] + extra

    @pl.when(z > 0)
    def _():
        wait(recv_sem, 2, z_recv.at[pl.ds(0, chips - 1)])

    @pl.when(z == 0)
    def _():
        wait(recv_sem, 2, z_recv)
        for t in range(steps):
            extra = z_recv[chips - 1, t]
            for i in range(chips, chips - 1 + late):
                extra = extra + z_recv[i, t]
            z_recv[chips - 1, t] = extra

    @pl.when(z > 0)
    def _():
        for t in range(steps):
            z_recv[chips - 1, t] = jnp.zeros_like(v_ref)

    for i in range(chips):
        current = [current[t] + z_recv[i, t] for t in range(steps)]

    potential = v_ref[...]
    for t in range(later):
        potential = leak_ref[...] * potential * (1.0 - spikes_ref[t].astype(F32)) + current[t]
    held_ref[...] = leak_ref[...] * potential * (1.0 - spikes_ref[later].astype(F32))
    last_ref[...] = current[later]

    wait(send_sem, 0, sib_recv)
    wait(send_sem, 1, x_recv)

    @pl.when(is_late)
    def _():
        wait(send_sem, 2, z_recv.at[pl.ds(0, chips)])

    @pl.when(jnp.logical_not(is_late))
    def _():
        wait(send_sem, 2, z_recv.at[pl.ds(0, chips - 1)])

    wait(send_sem, 3, y_recv)


def body(areas, secs, spikes, intra_weight, intra_dest, inter_weight, inter_target, v_init, leak):
    _, blocks, fan, width, _ = intra_weight.shape
    fan_areas = inter_weight.shape[2]
    steps = spikes.shape[1]
    chips = secs // CORES
    assert areas == SIDE * SIDE
    hbm = pl.BlockSpec(memory_space=pltpu.HBM)
    tile = (blocks, width)
    held, last = pl.pallas_call(
        kernel,
        out_shape=[jax.ShapeDtypeStruct(tile, F32)] * 2,
        in_specs=[hbm] * 7,
        out_specs=[pl.BlockSpec(memory_space=pltpu.VMEM)] * 2,
        scratch_shapes=[
            pltpu.VMEM((steps,) + tile, jnp.int32),
            pltpu.VMEM((fan, width), jnp.int32),
            pltpu.VMEM((fan_areas, areas), jnp.int32),
            pltpu.VMEM(tile, F32),
            pltpu.VMEM(tile, F32),
            pltpu.VMEM((blocks, fan, width, width), F32),
            pltpu.VMEM((blocks, fan_areas, width, width), F32),
            pltpu.VMEM((fan * blocks * 8, width), F32),
            pltpu.VMEM((fan_areas, blocks * 8, width), F32),
            pltpu.VMEM((CORES, chips, steps) + tile, F32),
            pltpu.VMEM((chips, steps) + tile, F32),
            pltpu.VMEM((chips, steps) + tile, F32),
            pltpu.VMEM((chips - 1 + chips // 2, steps) + tile, F32),
            pltpu.VMEM((SIDE, SIDE, steps - 1) + tile, F32),
            pltpu.VMEM((SIDE - 1, SIDE, steps - 1) + tile, F32),
            pltpu.VMEM((SIDE, steps - 1) + tile, F32),
            pltpu.VMEM((SIDE - 1, steps - 1) + tile, F32),
            pltpu.SemaphoreType.DMA((5,)),
            pltpu.SemaphoreType.DMA((HALVES + 1,)),
            pltpu.SemaphoreType.DMA((4,)),
            pltpu.SemaphoreType.DMA((4,)),
            pltpu.SemaphoreType.REGULAR((3,)),
        ],
        compiler_params=pltpu.CompilerParams(
            collective_id=0, has_side_effects=True, vmem_limit_bytes=16 << 20
        ),
    )(*(
        pltpu.with_memory_space_constraint(operand, pltpu.HBM)
        for operand in (
            spikes.reshape((steps,) + tile),
            intra_dest[0].T,
            inter_target[:, 0, :].T,
            v_init.reshape(tile),
            leak.reshape(tile),
            intra_weight[0],
            inter_weight[0],
        )
    ))
    return (held + last).reshape(1, blocks * width)


def solution(mesh):
    in_specs = (
        P("area", None, "sec"),
        P("area", "sec", None, None, None),
        P("area", None, None),
        P("area", "sec", None, None, None),
        P(None, "sec", None),
        P("area", "sec"),
        P("area", "sec"),
    )
    out_specs = P("area", "sec")
    run = functools.partial(body, mesh.shape["area"], mesh.shape["sec"])
    return jax.shard_map(run, mesh=mesh, in_specs=in_specs, out_specs=out_specs, check_vma=False)
```

```python
import functools

import jax
import jax.numpy as jnp
from jax import lax
from jax.experimental import pallas as pl
from jax.experimental.pallas import tpu as pltpu
from jax.sharding import PartitionSpec as P

MESH = pl.DeviceIdType.MESH
F32 = jnp.float32
BF16 = jnp.bfloat16
SIDE = 4
PARTS = 4
INTER_PARTS = 1
CORES = 2


def split(values):
    high = values.astype(BF16)
    low = (values - high.astype(F32)).astype(BF16)
    return high, low


def kernel(
    spikes_hbm, dest_hbm, target_hbm, v_hbm, leak_hbm, intra_hbm, inter_hbm,
    held_ref, last_ref,
    spikes_ref, dest_ref, target_ref, v_ref, leak_ref, intra_buf, inter_buf,
    intra_rows, inter_rows, intra_send, sib_recv, z_send, z_recv,
    x_send, x_recv, y_send, y_recv,
    small_sem, load_sem, send_sem, recv_sem, ready_sem,
):
    steps, blocks, width = spikes_ref.shape
    fan = intra_buf.shape[1]
    fan_areas = inter_buf.shape[1]
    chips = z_send.shape[0]
    later = steps - 1
    me_area = lax.axis_index("area")
    me_sec = lax.axis_index("sec")
    x, y = me_area // SIDE, me_area % SIDE
    z, core = me_sec // CORES, me_sec % CORES

    def at(dx=0, dy=0, dz=0, other=False):
        area = lax.rem(x + dx, SIDE) * SIDE + lax.rem(y + dy, SIDE)
        sec = lax.rem(z + dz, chips) * CORES + (1 - core if other else core)
        return {"area": area, "sec": sec}

    at_corner = x + y == 0

    late = chips // 2
    is_late = z >= late

    far_z = sorted(range(1, chips), key=lambda d: -min(d, chips - d))
    axes = (
        (z, chips, far_z, lambda d: at(dz=d)),
        (x, SIDE, (2, 1, 3), lambda d: at(dx=d)),
        (y, SIDE, (2, 1, 3), lambda d: at(dy=d)),
    )

    def partners(axis, after, act):
        place, length, distances, peer = axes[axis]
        for d in distances if after else sorted(distances):
            follows = place + d < length

            @pl.when(follows if after else jnp.logical_not(follows))
            def _():
                act(d, peer(d))

    def small(i):
        src = (spikes_hbm, dest_hbm, target_hbm, v_hbm, leak_hbm)[i]
        dst = (spikes_ref, dest_ref, target_ref, v_ref, leak_ref)[i]
        return pltpu.make_async_copy(src, dst, small_sem.at[i])

    def load(k):
        src, dst, parts, i = intra_hbm, intra_buf, PARTS, k
        if k >= PARTS:
            src, dst, parts, i = inter_hbm, inter_buf, INTER_PARTS, k - PARTS
        part = pl.ds(i * (blocks // parts), blocks // parts)
        return pltpu.make_async_copy(src.at[part], dst.at[part], load_sem.at[k])

    def remote(i, src, dst, peer):
        return pltpu.make_async_remote_copy(
            src_ref=src, dst_ref=dst, send_sem=send_sem.at[i], recv_sem=recv_sem.at[i],
            device_id=peer, device_id_type=MESH,
        )

    def wait(sem, i, ref):
        pltpu.make_async_copy(ref, ref, sem.at[i]).wait()

    def send_x(d, peer):
        remote(1, x_send.at[lax.rem(x + d, SIDE)], x_recv.at[d - 1], peer).start()

    def send_z(d, peer):
        remote(2, z_send.at[lax.rem(z + d, chips)], z_recv.at[d - 1], peer).start()

    def send_y(d, peer):
        remote(3, y_send.at[lax.rem(y + d, SIDE)], y_recv.at[d - 1], peer).start()

    def entered(axis):
        place, length, _, _ = axes[axis]

        @pl.when(place < length - 1)
        def _():
            pl.semaphore_wait(ready_sem.at[axis], length - 1 - place)

    for k, priority in ((0, 0), (1, 1), (2, 0), (3, 1), (4, 0)):
        load(k).start(priority=priority)
    for i in range(3):
        small(i).start()
    barrier = pltpu.get_barrier_semaphore()
    for axis in range(3):
        partners(axis, True, lambda d, peer: pl.semaphore_signal(barrier, inc=1, device_id=peer, device_id_type=MESH))
    pl.semaphore_signal(barrier, inc=1, device_id=at(other=True), device_id_type=MESH)

    @pl.when(z == 0)
    def _():
        for d in range(late, chips):
            pl.semaphore_signal(barrier, inc=1, device_id=at(dz=d, other=True), device_id_type=MESH)

    for i in range(3, 5):
        small(i).start()

    pl.semaphore_wait(barrier, 1 + x + y + z + z // late)
    for axis in range(3):
        ready = ready_sem.at[axis]
        partners(axis, False, lambda d, peer: pl.semaphore_signal(ready, inc=1, device_id=peer, device_id_type=MESH))

    for i in range(3):
        small(i).wait()
    lane = lax.broadcasted_iota(jnp.int32, (fan, width), 1)
    row = lax.broadcasted_iota(jnp.int32, (fan, width), 0)
    dest = pltpu.roll(dest_ref[...], lax.rem(width - me_sec * blocks, width), 1)
    dest = pltpu.roll(dest, 0, 1, stride=blocks, stride_axis=0)
    dest = jnp.sum(jnp.where(lane // blocks == row, dest, 0), axis=0, keepdims=True)
    half = fan * blocks
    dest = dest + pltpu.roll(dest, half, 1)
    grid_row = lax.broadcasted_iota(jnp.int32, (width, width), 0)
    picker = jnp.where(grid_row == dest, 1.0, 0.0).astype(BF16)
    target_lane = lax.broadcasted_iota(jnp.int32, target_ref.shape, 1)
    target = jnp.sum(jnp.where(target_lane == me_area, target_ref[...], 0), axis=1, keepdims=True)
    targets = [jnp.broadcast_to(target[j:j + 1], (blocks, width)) for j in range(fan_areas)]

    def spikes_of(k):
        rows = spikes_ref[:, k, :].astype(F32).astype(BF16)
        rows = jnp.concatenate([rows, jnp.zeros((8 - steps, width), BF16)], axis=0)
        return jnp.concatenate([rows, rows], axis=1)

    def products(k, left, right):
        high, low = split(jnp.concatenate([left, right], axis=1))
        rhs = jnp.concatenate([high, low], axis=0)
        part = jnp.dot(spikes_of(k), rhs, preferred_element_type=F32)
        return part[:, :width], part[:, width:]

    def inter():
        for k in range(INTER_PARTS):
            load(PARTS + k).wait()
        for k in range(blocks):
            parts = products(k, inter_buf[k, 0], inter_buf[k, 1])
            for j in range(fan_areas):
                inter_rows[j, pl.ds(k * 8, 8), :] = parts[j]
        for t in range(later):
            rows = [inter_rows[j, pl.ds(t, blocks, stride=8), :] for j in range(fan_areas)]
            for b in range(SIDE * SIDE):
                total = jnp.where(targets[0] == b, rows[0], 0.0)
                for j in range(1, fan_areas):
                    total = jnp.where(targets[j] == b, rows[j], total)
                x_send[b // SIDE, b % SIDE, t] = total


    def intra(k):
        for f in range(0, fan, 2):
            left, right = products(k, intra_buf[k, f], intra_buf[k, f + 1])
            intra_rows[pl.ds((f * blocks + k) * 8, 8), :] = left
            intra_rows[pl.ds(((f + 1) * blocks + k) * 8, 8), :] = right

    @pl.when(jnp.logical_not(at_corner))
    def _():
        inter()
        partners(1, False, send_x)

    for k in range(PARTS // 2):
        load(k).wait()
    for k in range(blocks // 2):
        intra(k)

    for k in range(PARTS // 2, PARTS):
        load(k).wait()
    for k in range(blocks // 2, blocks):
        intra(k)
    for t in range(steps):
        high, low = split(intra_rows[pl.ds(t, half, stride=8), :])
        grid = jnp.dot(picker, jnp.concatenate([high, low], axis=0), preferred_element_type=F32)
        for p in range(chips * CORES):
            intra_send[p % CORES, p // CORES, t] = grid[p * blocks:(p + 1) * blocks, :]


    @pl.when(is_late)
    def _():
        back = chips - z
        remote(2, intra_send.at[core, 0], z_recv.at[back - 1], at(dz=back)).start()
        remote(2, intra_send.at[1 - core, 0], z_recv.at[chips - 2 + back], at(dz=back, other=True)).start()

    remote(0, intra_send.at[1 - core], sib_recv, at(other=True)).start()

    @pl.when(at_corner)
    def _():
        inter()


    wait(recv_sem, 0, sib_recv)
    for p in range(chips):
        for t in range(steps):
            z_send[p, t] = intra_send[core, p, t] + sib_recv[p, t]
    def send_z_summed(d, peer):
        @pl.when(jnp.logical_not(jnp.logical_and(is_late, z + d == chips)))
        def _():
            send_z(d, peer)

    partners(0, False, send_z_summed)
    entered(1)
    partners(1, True, send_x)

    wait(recv_sem, 1, x_recv)
    for b in range(SIDE):
        for t in range(later):
            y_send[b, t] = x_send[x, b, t] + x_recv[0, b, t] + x_recv[1, b, t] + x_recv[2, b, t]
    partners(2, False, send_y)
    entered(0)
    partners(0, True, send_z)
    entered(2)
    partners(2, True, send_y)

    for i in range(3, 5):
        small(i).wait()
    wait(recv_sem, 3, y_recv)
    current = [z_send[z, t] for t in range(steps)]
    for t in range(later):
        extra = y_send[y, t]
        for i in range(SIDE - 1):
            extra = extra + y_recv[i, t]
        current[t + 1] = current[t + 1] + extra

    @pl.when(z > 0)
    def _():
        wait(recv_sem, 2, z_recv.at[pl.ds(0, chips - 1)])

    @pl.when(z == 0)
    def _():
        wait(recv_sem, 2, z_recv)
        for t in range(steps):
            extra = z_recv[chips - 1, t]
            for i in range(chips, chips - 1 + late):
                extra = extra + z_recv[i, t]
            z_recv[chips - 1, t] = extra

    @pl.when(z > 0)
    def _():
        for t in range(steps):
            z_recv[chips - 1, t] = jnp.zeros_like(v_ref)

    for i in range(chips):
        current = [current[t] + z_recv[i, t] for t in range(steps)]

    potential = v_ref[...]
    for t in range(later):
        potential = leak_ref[...] * potential * (1.0 - spikes_ref[t].astype(F32)) + current[t]
    held_ref[...] = leak_ref[...] * potential * (1.0 - spikes_ref[later].astype(F32))
    last_ref[...] = current[later]

    wait(send_sem, 0, sib_recv)
    wait(send_sem, 1, x_recv)

    @pl.when(is_late)
    def _():
        wait(send_sem, 2, z_recv.at[pl.ds(0, chips)])

    @pl.when(jnp.logical_not(is_late))
    def _():
        wait(send_sem, 2, z_recv.at[pl.ds(0, chips - 1)])

    wait(send_sem, 3, y_recv)


def body(areas, secs, spikes, intra_weight, intra_dest, inter_weight, inter_target, v_init, leak):
    _, blocks, fan, width, _ = intra_weight.shape
    fan_areas = inter_weight.shape[2]
    steps = spikes.shape[1]
    chips = secs // CORES
    assert areas == SIDE * SIDE
    hbm = pl.BlockSpec(memory_space=pltpu.HBM)
    tile = (blocks, width)
    held, last = pl.pallas_call(
        kernel,
        out_shape=[jax.ShapeDtypeStruct(tile, F32)] * 2,
        in_specs=[hbm] * 7,
        out_specs=[pl.BlockSpec(memory_space=pltpu.VMEM)] * 2,
        scratch_shapes=[
            pltpu.VMEM((steps,) + tile, jnp.int32),
            pltpu.VMEM((fan, width), jnp.int32),
            pltpu.VMEM((fan_areas, areas), jnp.int32),
            pltpu.VMEM(tile, F32),
            pltpu.VMEM(tile, F32),
            pltpu.VMEM((blocks, fan, width, width), F32),
            pltpu.VMEM((blocks, fan_areas, width, width), F32),
            pltpu.VMEM((fan * blocks * 8, width), F32),
            pltpu.VMEM((fan_areas, blocks * 8, width), F32),
            pltpu.VMEM((CORES, chips, steps) + tile, F32),
            pltpu.VMEM((chips, steps) + tile, F32),
            pltpu.VMEM((chips, steps) + tile, F32),
            pltpu.VMEM((chips - 1 + chips // 2, steps) + tile, F32),
            pltpu.VMEM((SIDE, SIDE, steps - 1) + tile, F32),
            pltpu.VMEM((SIDE - 1, SIDE, steps - 1) + tile, F32),
            pltpu.VMEM((SIDE, steps - 1) + tile, F32),
            pltpu.VMEM((SIDE - 1, steps - 1) + tile, F32),
            pltpu.SemaphoreType.DMA((5,)),
            pltpu.SemaphoreType.DMA((PARTS + INTER_PARTS,)),
            pltpu.SemaphoreType.DMA((4,)),
            pltpu.SemaphoreType.DMA((4,)),
            pltpu.SemaphoreType.REGULAR((3,)),
        ],
        compiler_params=pltpu.CompilerParams(
            collective_id=0, has_side_effects=True, vmem_limit_bytes=16 << 20
        ),
    )(*(
        pltpu.with_memory_space_constraint(operand, pltpu.HBM)
        for operand in (
            spikes.reshape((steps,) + tile),
            intra_dest[0].T,
            inter_target[:, 0, :].T,
            v_init.reshape(tile),
            leak.reshape(tile),
            intra_weight[0],
            inter_weight[0],
        )
    ))
    return (held + last).reshape(1, blocks * width)


def solution(mesh):
    in_specs = (
        P("area", None, "sec"),
        P("area", "sec", None, None, None),
        P("area", None, None),
        P("area", "sec", None, None, None),
        P(None, "sec", None),
        P("area", "sec"),
        P("area", "sec"),
    )
    out_specs = P("area", "sec")
    run = functools.partial(body, mesh.shape["area"], mesh.shape["sec"])
    return jax.shard_map(run, mesh=mesh, in_specs=in_specs, out_specs=out_specs, check_vma=False)
```

```python
import functools

import jax
import jax.numpy as jnp
from jax import lax
from jax.experimental import pallas as pl
from jax.experimental.pallas import tpu as pltpu
from jax.sharding import PartitionSpec as P

MESH = pl.DeviceIdType.MESH
F32 = jnp.float32
BF16 = jnp.bfloat16
SIDE = 4
PARTS = 4
INTER_PARTS = 1
CORES = 2


def split(values):
    high = values.astype(BF16)
    low = (values - high.astype(F32)).astype(BF16)
    return high, low


def kernel(
    spikes_hbm, dest_hbm, target_hbm, v_hbm, leak_hbm, intra_hbm, inter_hbm,
    held_ref, last_ref,
    spikes_ref, dest_ref, target_ref, v_ref, leak_ref, intra_buf, inter_buf,
    intra_rows, inter_rows, intra_send, sib_recv, z_send, z_recv,
    x_send, x_recv, y_send, y_recv,
    small_sem, load_sem, send_sem, recv_sem, ready_sem,
):
    steps, blocks, width = spikes_ref.shape
    fan = intra_buf.shape[1]
    fan_areas = inter_buf.shape[1]
    chips = z_send.shape[0]
    later = steps - 1
    me_area = lax.axis_index("area")
    me_sec = lax.axis_index("sec")
    x, y = me_area // SIDE, me_area % SIDE
    z, core = me_sec // CORES, me_sec % CORES

    def at(dx=0, dy=0, dz=0, other=False):
        area = lax.rem(x + dx, SIDE) * SIDE + lax.rem(y + dy, SIDE)
        sec = lax.rem(z + dz, chips) * CORES + (1 - core if other else core)
        return {"area": area, "sec": sec}

    at_corner = x + y == 0

    late = chips // 2
    is_late = z >= late

    far_z = sorted(range(1, chips), key=lambda d: -min(d, chips - d))
    axes = (
        (z, chips, far_z, lambda d: at(dz=d)),
        (x, SIDE, (2, 1, 3), lambda d: at(dx=d)),
        (y, SIDE, (2, 1, 3), lambda d: at(dy=d)),
    )

    def partners(axis, after, act):
        place, length, distances, peer = axes[axis]
        for d in distances if after else sorted(distances):
            follows = place + d < length

            @pl.when(follows if after else jnp.logical_not(follows))
            def _():
                act(d, peer(d))

    def small(i):
        src = (spikes_hbm, dest_hbm, target_hbm, v_hbm, leak_hbm)[i]
        dst = (spikes_ref, dest_ref, target_ref, v_ref, leak_ref)[i]
        return pltpu.make_async_copy(src, dst, small_sem.at[i])

    def load(k):
        src, dst, parts, i = intra_hbm, intra_buf, PARTS, k
        if k >= PARTS:
            src, dst, parts, i = inter_hbm, inter_buf, INTER_PARTS, k - PARTS
        part = pl.ds(i * (blocks // parts), blocks // parts)
        return pltpu.make_async_copy(src.at[part], dst.at[part], load_sem.at[k])

    def remote(i, src, dst, peer):
        return pltpu.make_async_remote_copy(
            src_ref=src, dst_ref=dst, send_sem=send_sem.at[i], recv_sem=recv_sem.at[i],
            device_id=peer, device_id_type=MESH,
        )

    def wait(sem, i, ref):
        pltpu.make_async_copy(ref, ref, sem.at[i]).wait()

    def send_x(d, peer):
        remote(1, x_send.at[lax.rem(x + d, SIDE)], x_recv.at[d - 1], peer).start()

    def send_z(d, peer):
        remote(2, z_send.at[lax.rem(z + d, chips)], z_recv.at[d - 1], peer).start()

    def send_y(d, peer):
        remote(3, y_send.at[lax.rem(y + d, SIDE)], y_recv.at[d - 1], peer).start()

    def entered(axis):
        place, length, _, _ = axes[axis]

        @pl.when(place < length - 1)
        def _():
            pl.semaphore_wait(ready_sem.at[axis], length - 1 - place)

    for k, priority in ((0, 0), (1, 1), (2, 0), (3, 1)):
        load(k).start(priority=priority)
    @pl.when(jnp.logical_not(at_corner))
    def _():
        load(PARTS).start()

    for i in range(3):
        small(i).start()
    barrier = pltpu.get_barrier_semaphore()
    for axis in range(3):
        partners(axis, True, lambda d, peer: pl.semaphore_signal(barrier, inc=1, device_id=peer, device_id_type=MESH))
    pl.semaphore_signal(barrier, inc=1, device_id=at(other=True), device_id_type=MESH)

    @pl.when(z == 0)
    def _():
        for d in range(late, chips):
            pl.semaphore_signal(barrier, inc=1, device_id=at(dz=d, other=True), device_id_type=MESH)

    for i in range(3, 5):
        small(i).start()

    pl.semaphore_wait(barrier, 1 + x + y + z + z // late)
    for axis in range(3):
        ready = ready_sem.at[axis]
        partners(axis, False, lambda d, peer: pl.semaphore_signal(ready, inc=1, device_id=peer, device_id_type=MESH))

    for i in range(3):
        small(i).wait()
    lane = lax.broadcasted_iota(jnp.int32, (fan, width), 1)
    row = lax.broadcasted_iota(jnp.int32, (fan, width), 0)
    dest = pltpu.roll(dest_ref[...], lax.rem(width - me_sec * blocks, width), 1)
    dest = pltpu.roll(dest, 0, 1, stride=blocks, stride_axis=0)
    dest = jnp.sum(jnp.where(lane // blocks == row, dest, 0), axis=0, keepdims=True)
    half = fan * blocks
    dest = dest + pltpu.roll(dest, half, 1)
    grid_row = lax.broadcasted_iota(jnp.int32, (width, width), 0)
    picker = jnp.where(grid_row == dest, 1.0, 0.0).astype(BF16)
    target_lane = lax.broadcasted_iota(jnp.int32, target_ref.shape, 1)
    target = jnp.sum(jnp.where(target_lane == me_area, target_ref[...], 0), axis=1, keepdims=True)
    targets = [jnp.broadcast_to(target[j:j + 1], (blocks, width)) for j in range(fan_areas)]

    def spikes_of(k):
        rows = spikes_ref[:, k, :].astype(F32).astype(BF16)
        rows = jnp.concatenate([rows, jnp.zeros((8 - steps, width), BF16)], axis=0)
        return jnp.concatenate([rows, rows], axis=1)

    def products(k, left, right):
        high, low = split(jnp.concatenate([left, right], axis=1))
        rhs = jnp.concatenate([high, low], axis=0)
        part = jnp.dot(spikes_of(k), rhs, preferred_element_type=F32)
        return part[:, :width], part[:, width:]

    def inter():
        for k in range(INTER_PARTS):
            load(PARTS + k).wait()
        for k in range(blocks):
            parts = products(k, inter_buf[k, 0], inter_buf[k, 1])
            for j in range(fan_areas):
                inter_rows[j, pl.ds(k * 8, 8), :] = parts[j]
        for t in range(later):
            rows = [inter_rows[j, pl.ds(t, blocks, stride=8), :] for j in range(fan_areas)]
            for b in range(SIDE * SIDE):
                total = jnp.where(targets[0] == b, rows[0], 0.0)
                for j in range(1, fan_areas):
                    total = jnp.where(targets[j] == b, rows[j], total)
                x_send[b // SIDE, b % SIDE, t] = total


    def intra(k):
        for f in range(0, fan, 2):
            left, right = products(k, intra_buf[k, f], intra_buf[k, f + 1])
            intra_rows[pl.ds((f * blocks + k) * 8, 8), :] = left
            intra_rows[pl.ds(((f + 1) * blocks + k) * 8, 8), :] = right

    @pl.when(jnp.logical_not(at_corner))
    def _():
        inter()
        partners(1, False, send_x)

    for k in range(PARTS // 2):
        load(k).wait()

    @pl.when(at_corner)
    def _():
        load(PARTS).start()

    for k in range(blocks // 2):
        intra(k)

    for k in range(PARTS // 2, PARTS):
        load(k).wait()
    for k in range(blocks // 2, blocks):
        intra(k)
    for t in range(steps):
        high, low = split(intra_rows[pl.ds(t, half, stride=8), :])
        grid = jnp.dot(picker, jnp.concatenate([high, low], axis=0), preferred_element_type=F32)
        for p in range(chips * CORES):
            intra_send[p % CORES, p // CORES, t] = grid[p * blocks:(p + 1) * blocks, :]


    @pl.when(is_late)
    def _():
        back = chips - z
        remote(2, intra_send.at[core, 0], z_recv.at[back - 1], at(dz=back)).start()
        remote(2, intra_send.at[1 - core, 0], z_recv.at[chips - 2 + back], at(dz=back, other=True)).start()

    remote(0, intra_send.at[1 - core], sib_recv, at(other=True)).start()

    @pl.when(at_corner)
    def _():
        inter()


    wait(recv_sem, 0, sib_recv)
    for p in range(chips):
        for t in range(steps):
            z_send[p, t] = intra_send[core, p, t] + sib_recv[p, t]
    def send_z_summed(d, peer):
        @pl.when(jnp.logical_not(jnp.logical_and(is_late, z + d == chips)))
        def _():
            send_z(d, peer)

    partners(0, False, send_z_summed)
    entered(1)
    partners(1, True, send_x)

    wait(recv_sem, 1, x_recv)
    for b in range(SIDE):
        for t in range(later):
            y_send[b, t] = x_send[x, b, t] + x_recv[0, b, t] + x_recv[1, b, t] + x_recv[2, b, t]
    partners(2, False, send_y)
    entered(0)
    partners(0, True, send_z)
    entered(2)
    partners(2, True, send_y)

    for i in range(3, 5):
        small(i).wait()
    wait(recv_sem, 3, y_recv)
    current = [z_send[z, t] for t in range(steps)]
    for t in range(later):
        extra = y_send[y, t]
        for i in range(SIDE - 1):
            extra = extra + y_recv[i, t]
        current[t + 1] = current[t + 1] + extra

    @pl.when(z > 0)
    def _():
        wait(recv_sem, 2, z_recv.at[pl.ds(0, chips - 1)])

    @pl.when(z == 0)
    def _():
        wait(recv_sem, 2, z_recv)
        for t in range(steps):
            extra = z_recv[chips - 1, t]
            for i in range(chips, chips - 1 + late):
                extra = extra + z_recv[i, t]
            z_recv[chips - 1, t] = extra

    @pl.when(z > 0)
    def _():
        for t in range(steps):
            z_recv[chips - 1, t] = jnp.zeros_like(v_ref)

    for i in range(chips):
        current = [current[t] + z_recv[i, t] for t in range(steps)]

    potential = v_ref[...]
    for t in range(later):
        potential = leak_ref[...] * potential * (1.0 - spikes_ref[t].astype(F32)) + current[t]
    held_ref[...] = leak_ref[...] * potential * (1.0 - spikes_ref[later].astype(F32))
    last_ref[...] = current[later]

    wait(send_sem, 0, sib_recv)
    wait(send_sem, 1, x_recv)

    @pl.when(is_late)
    def _():
        wait(send_sem, 2, z_recv.at[pl.ds(0, chips)])

    @pl.when(jnp.logical_not(is_late))
    def _():
        wait(send_sem, 2, z_recv.at[pl.ds(0, chips - 1)])

    wait(send_sem, 3, y_recv)


def body(areas, secs, spikes, intra_weight, intra_dest, inter_weight, inter_target, v_init, leak):
    _, blocks, fan, width, _ = intra_weight.shape
    fan_areas = inter_weight.shape[2]
    steps = spikes.shape[1]
    chips = secs // CORES
    assert areas == SIDE * SIDE
    hbm = pl.BlockSpec(memory_space=pltpu.HBM)
    tile = (blocks, width)
    held, last = pl.pallas_call(
        kernel,
        out_shape=[jax.ShapeDtypeStruct(tile, F32)] * 2,
        in_specs=[hbm] * 7,
        out_specs=[pl.BlockSpec(memory_space=pltpu.VMEM)] * 2,
        scratch_shapes=[
            pltpu.VMEM((steps,) + tile, jnp.int32),
            pltpu.VMEM((fan, width), jnp.int32),
            pltpu.VMEM((fan_areas, areas), jnp.int32),
            pltpu.VMEM(tile, F32),
            pltpu.VMEM(tile, F32),
            pltpu.VMEM((blocks, fan, width, width), F32),
            pltpu.VMEM((blocks, fan_areas, width, width), F32),
            pltpu.VMEM((fan * blocks * 8, width), F32),
            pltpu.VMEM((fan_areas, blocks * 8, width), F32),
            pltpu.VMEM((CORES, chips, steps) + tile, F32),
            pltpu.VMEM((chips, steps) + tile, F32),
            pltpu.VMEM((chips, steps) + tile, F32),
            pltpu.VMEM((chips - 1 + chips // 2, steps) + tile, F32),
            pltpu.VMEM((SIDE, SIDE, steps - 1) + tile, F32),
            pltpu.VMEM((SIDE - 1, SIDE, steps - 1) + tile, F32),
            pltpu.VMEM((SIDE, steps - 1) + tile, F32),
            pltpu.VMEM((SIDE - 1, steps - 1) + tile, F32),
            pltpu.SemaphoreType.DMA((5,)),
            pltpu.SemaphoreType.DMA((PARTS + INTER_PARTS,)),
            pltpu.SemaphoreType.DMA((4,)),
            pltpu.SemaphoreType.DMA((4,)),
            pltpu.SemaphoreType.REGULAR((3,)),
        ],
        compiler_params=pltpu.CompilerParams(
            collective_id=0, has_side_effects=True, vmem_limit_bytes=16 << 20
        ),
    )(*(
        pltpu.with_memory_space_constraint(operand, pltpu.HBM)
        for operand in (
            spikes.reshape((steps,) + tile),
            intra_dest[0].T,
            inter_target[:, 0, :].T,
            v_init.reshape(tile),
            leak.reshape(tile),
            intra_weight[0],
            inter_weight[0],
        )
    ))
    return (held + last).reshape(1, blocks * width)


def solution(mesh):
    in_specs = (
        P("area", None, "sec"),
        P("area", "sec", None, None, None),
        P("area", None, None),
        P("area", "sec", None, None, None),
        P(None, "sec", None),
        P("area", "sec"),
        P("area", "sec"),
    )
    out_specs = P("area", "sec")
    run = functools.partial(body, mesh.shape["area"], mesh.shape["sec"])
    return jax.shard_map(run, mesh=mesh, in_specs=in_specs, out_specs=out_specs, check_vma=False)
```
